128 devices in a mesh: tm: 8 (over z_lo, x), head: 16 (over y, z_hi, core).
Axes of the slice: x: 4, y: 4, z: 4 (z_hi: 2, z_lo: 2; z = z_hi * 2 + z_lo), core: 2. Of those that a mesh axis runs over, the one named last changes fastest.
Arguments:
- queries: bfloat16 [12288, 4096], P(('tm', 'head')), may hold values from -6 to 6
- key_tokens: bfloat16 [12288, 4096], P(('tm', 'head')), may hold values from -6 to 6
- value_tokens: bfloat16 [12288, 4096], P(('tm', 'head')), may hold values from -6 to 6
- outputs: bfloat16 [12288, 4096], P(('tm', 'head')), may hold values from -6 to 6
- out_grad: bfloat16 [12288, 4096], P(('tm', 'head')), may hold values from -96 to 96
- log_sum: float32 [12288, 32], P('tm', 'head'), may hold values from 7 to 9
- neighbours: int32 [96, 27], replicated, may hold values from -1 to 95, as said below
Outputs:
- query_grad: bfloat16 [12288, 4096], P(('tm', 'head'))
- key_grad: bfloat16 [12288, 4096], P(('tm', 'head'))
- value_grad: bfloat16 [12288, 4096], P(('tm', 'head'))
The draws below stay inside these ranges and needn't reach their ends.
Inputs may be any that keep to these rules, and one draw needn't show every extreme that they name: `neighbours`: tile t lies in frame f = t // 12, tile row r and tile column c of that frame's grid of 3 x 4 tiles (rows major). Slot 9 a + 3 b + e of row t (a, b, e in 0, 1, 2) names the tile of frame f + a - 1, row r0 + b - 1, column c0 + e - 1, where the window centre (r0, c0) lies within one row and one column of (r, c) and the 3 x 3 window lies wholly inside the frame; the slot holds -1 exactly where frame f + a - 1 is outside the video.
All inputs are finite; a program needn't handle non-finite values.
Results may differ from the reference program's by a relative error of at most 0.0067.
Values may be sent and summed in bfloat16 or wider, within the bound.
A program may use at most 192 MiB of HBM per device.

```python
import jax
import jax.numpy as jnp
from jax import lax

HD = 128
TILE = 128
FRAME_ROWS = 3
FRAME_COLS = 4
HEADS = 32
FEAT = 4096
TILES = 96
TOKENS = 12288


def draw_neighbours(key, part):
    frame_tiles = FRAME_ROWS * FRAME_COLS
    frame_count = TILES // frame_tiles
    tile_ids = jnp.arange(TILES, dtype=jnp.int32)
    frame = tile_ids // frame_tiles
    row_ids = tile_ids % frame_tiles // FRAME_COLS
    col_ids = tile_ids % FRAME_COLS
    shifts = jax.random.randint(key, (TILES, 2), -1, 2, dtype=jnp.int32)
    centre_row = jnp.clip(row_ids + shifts[:, 0], 1, FRAME_ROWS - 2)
    centre_col = jnp.clip(col_ids + shifts[:, 1], 1, FRAME_COLS - 2)
    slot_ids = jnp.arange(27, dtype=jnp.int32)
    step_frame = slot_ids // 9 - 1
    step_row = slot_ids // 3 % 3 - 1
    step_col = slot_ids % 3 - 1
    target_frame = frame[:, None] + step_frame[None, :]
    target_row = centre_row[:, None] + step_row[None, :]
    target_col = centre_col[:, None] + step_col[None, :]
    target = target_frame * frame_tiles + target_row * FRAME_COLS + target_col
    inside = (target_frame >= 0) & (target_frame < frame_count)
    return jnp.where(inside, target, -1).astype(jnp.int32)


def shard_levels(rng, extent, shards, smallest, largest):
    factor_of, own = 1.0, jax.random.fold_in(rng, 6)
    for dim, blocks in shards:
        draws = jnp.exp(jax.random.uniform(jax.random.fold_in(own, dim), (blocks,), jnp.float32, smallest / len(shards), largest / len(shards)))
        factor_of = factor_of * jnp.repeat(draws, extent[dim] // blocks).reshape([-1 if axis == dim else 1 for axis in range(len(extent))])
    return factor_of


def normal_values(own_key, extent, scale, most, pieces=(), kind=jnp.bfloat16):
    gain = shard_levels(own_key, extent, pieces, -0.22, 0.18) if pieces else 1.0
    result = jax.random.normal(own_key, extent, jnp.float32) * scale * gain
    return jnp.minimum(jnp.maximum(result, -most), most).astype(kind)


def setup_inputs(seed: int = 0) -> dict:
    seeds = jax.random.split(jax.random.key(seed), 8)
    queries = normal_values(seeds[0], (TOKENS, FEAT), 1.0, 6.0, ((0, 128),))
    key_tokens = normal_values(seeds[1], (TOKENS, FEAT), 1.0, 6.0, ((0, 128),))
    value_tokens = normal_values(seeds[2], (TOKENS, FEAT), 1.0, 6.0, ((0, 128),))
    outputs = normal_values(seeds[3], (TOKENS, FEAT), 1.0, 6.0, ((0, 128),))
    out_grad = normal_values(seeds[4], (TOKENS, FEAT), 16.0, 96.0, ((0, 128),))
    log_sum = jnp.clip(7.0 + 2.0 * jax.random.uniform(seeds[5], (TOKENS, HEADS), jnp.float32) ** shard_levels(seeds[5], (TOKENS, HEADS), ((0, 8), (1, 16)), -0.2, 0.2), 7.0, 9.0)
    neighbours = draw_neighbours(jax.random.fold_in(seeds[7], 71), 0)
    return {"queries": queries, "key_tokens": key_tokens, "value_tokens": value_tokens, "outputs": outputs, "out_grad": out_grad, "log_sum": log_sum, "neighbours": neighbours}


def reference(queries, key_tokens, value_tokens, outputs, out_grad, log_sum, neighbours):
    tile_count = neighbours.shape[0]
    head_count = log_sum.shape[1]
    score_scale = HD ** -0.5
    highest = lax.Precision.HIGHEST
    shape_four = (tile_count, TILE, head_count, HD)
    query_tiles = queries.reshape(shape_four).astype(jnp.float32)
    key_tiles = key_tokens.reshape(shape_four).astype(jnp.float32)
    value_tiles = value_tokens.reshape(shape_four).astype(jnp.float32)
    grad_tiles = out_grad.reshape(shape_four).astype(jnp.float32)
    delta = jnp.sum(grad_tiles * outputs.reshape(shape_four).astype(jnp.float32), axis=3)
    stats = log_sum.reshape(tile_count, TILE, head_count)

    def visit_tile(totals, tile_index):
        key_total, value_total = totals
        listed = neighbours[tile_index]
        live = (listed >= 0).astype(jnp.float32)
        chosen = jnp.maximum(listed, 0).astype(jnp.int32)
        query_here = query_tiles[tile_index]
        grad_here = grad_tiles[tile_index]
        keys_near = key_tiles[chosen]
        values_near = value_tiles[chosen]
        scores = jnp.einsum('thd,nshd->htns', query_here, keys_near, precision=highest) * score_scale
        attn_weight = jnp.exp(scores - stats[tile_index].T[:, :, None, None]) * live[None, None, :, None]
        weight_low = lax.optimization_barrier(attn_weight.astype(jnp.bfloat16))
        prob_grad = jnp.einsum('thd,nshd->htns', grad_here, values_near, precision=highest)
        score_grad = (attn_weight * (prob_grad - delta[tile_index].T[:, :, None, None])).astype(jnp.bfloat16)
        score_grad = lax.optimization_barrier(score_grad)
        grad_wide = score_grad.astype(jnp.float32)
        weight_wide = weight_low.astype(jnp.float32)
        query_part = (jnp.einsum('htns,nshd->thd', grad_wide, keys_near, precision=highest) * score_scale).astype(jnp.bfloat16)
        key_part = jnp.einsum('htns,thd->nshd', grad_wide, query_here, precision=highest) * score_scale
        value_part = jnp.einsum('htns,thd->nshd', weight_wide, grad_here, precision=highest)
        return (key_total.at[chosen].add(key_part), value_total.at[chosen].add(value_part)), query_part

    empty_sum = jnp.zeros(shape_four, jnp.float32)
    totals, query_parts = lax.scan(visit_tile, (empty_sum, empty_sum), jnp.arange(tile_count, dtype=jnp.int32))
    token_count = tile_count * TILE
    feat_width = head_count * HD
    return (query_parts.reshape(token_count, feat_width),
            totals[0].reshape(token_count, feat_width).astype(jnp.bfloat16),
            totals[1].reshape(token_count, feat_width).astype(jnp.bfloat16))
```

```python
import functools

import jax
import jax.numpy as jnp
from jax import lax
from jax.experimental import pallas as pl
from jax.experimental.pallas import tpu as pltpu
from jax.sharding import PartitionSpec as P

HD = 128
FRAME = 1536
SLAB = 96
ROWS = 3
QROW = 512
HEADS = 32
LOG2E = 1.4426950408889634
SCALE = HD**-0.5
MESH = pl.DeviceIdType.MESH
NT = (((1,), (1,)), ((), ()))
NN = (((1,), (0,)), ((), ()))


def dot(left, right, dims):
    return lax.dot_general(left, right, dims, preferred_element_type=jnp.float32)


def kernel(
    q_hbm, k_hbm, v_hbm, o_hbm, g_hbm, lse_hbm, bias,
    dq_out, dk_out, dv_out,
    qb, gb, kb, vb, kt, dqt, dka, dva, stat,
    ob, gl, dl_src, dl, ls, part_src, part, oq, ok, ov,
    load_sem, in_send, in_recv, halo_send, halo_recv, part_send, part_recv, out_send, out_recv,
):
    tm, hd = lax.axis_index("tm"), lax.axis_index("head")
    z_lo, x = tm // 4, tm % 4
    y, z_hi, core = hd // 4, (hd // 2) % 2, hd % 2
    place = 2 * (1 - z_lo) + core
    head = y * 8 + z_hi * 4 + x
    slot = tm % 2

    def holder(n):
        return ((1 - n // 2) * 4 + x, y * 4 + z_hi * 2 + n % 2)

    lower, upper = holder((place + 3) % 4), holder((place + 1) % 4)
    has_lower, has_upper = place > 0, place < 3

    def target(h):
        return ((1 - z_lo) * 4 + h % 4, (h // 8) * 4 + ((h // 4) % 2) * 2 + x // 2)

    def source(j, s):
        return (2 * place + j, s)

    load_o = pltpu.make_async_copy(o_hbm, ob, load_sem.at[0])
    load_g = pltpu.make_async_copy(g_hbm, gl, load_sem.at[1])
    load_o.start()
    load_g.start()

    barrier = pltpu.get_barrier_semaphore()

    def greet(i, _):
        pl.semaphore_signal(barrier, inc=1, device_id=source(i // 16, i % 16), device_id_type=MESH)
        return 0

    lax.fori_loop(0, 32, greet, 0)
    for peer in (lower, upper):
        pl.semaphore_signal(barrier, inc=1, device_id=peer, device_id_type=MESH)
    pl.semaphore_wait(barrier, 34)

    def columns(h):
        return pl.ds(pl.multiple_of(h * HD, HD), HD)

    first = (slot * 16 + hd) * 5

    def spread(array, src, dst, row):
        def send(i, _):
            h = (i + first) % HEADS
            pltpu.make_async_remote_copy(
                src.at[:, columns(h)],
                dst.at[pl.ds(pl.multiple_of(row, 32), SLAB)],
                in_send.at[array], in_recv.at[array, slot],
                device_id=target(h), device_id_type=MESH,
            ).start()
            return 0

        lax.fori_loop(0, HEADS, send, 0)

    own_row = (1 + slot) * FRAME + hd * SLAB
    kv_row = slot * FRAME + hd * SLAB
    spread(0, q_hbm, qb, own_row)
    spread(1, g_hbm, gb, own_row)
    for i in range(2):
        pltpu.make_async_remote_copy(
            lse_hbm.at[i], ls.at[1 + slot], in_send.at[5], in_recv.at[5, slot],
            device_id=target(2 * hd + i), device_id_type=MESH,
        ).start()
    spread(2, k_hbm, kb, kv_row)
    spread(3, v_hbm, vb, kv_row)

    load_o.wait()
    load_g.wait()

    def delta(h, _):
        product = ob[:, columns(h)].astype(jnp.float32) * gl[:, columns(h)].astype(jnp.float32)
        tall = jnp.concatenate([product, jnp.zeros((HD - SLAB, HD), jnp.float32)], axis=0)
        row = jnp.sum(tall.T, axis=0, keepdims=True)
        dl_src[h] = jnp.broadcast_to(row, (8, HD))
        return 0

    lax.fori_loop(0, HEADS, delta, 0)

    def send_delta(i, _):
        h = (i + first) % HEADS
        pltpu.make_async_remote_copy(
            dl_src.at[h], dl.at[1 + slot, hd], in_send.at[4], in_recv.at[4, slot],
            device_id=target(h), device_id_type=MESH,
        ).start()
        return 0

    lax.fori_loop(0, HEADS, send_delta, 0)

    def frame(ref, j):
        return ref.at[j * FRAME : (j + 1) * FRAME]

    kinds = (
        (0, lambda s: frame(qb, s)),
        (1, lambda s: frame(gb, s)),
        (4, lambda s: dl.at[s]),
        (5, lambda s: ls.at[s]),
    )

    def arrived(array, j, view):
        pltpu.make_async_remote_copy(
            view, view, in_send.at[array], in_recv.at[array, j], device_id=lower, device_id_type=MESH
        ).wait_recv()

    def halo(i, j, view):
        return pltpu.make_async_remote_copy(
            view(1 + j), view(3 - 3 * j), halo_send.at[i, j], halo_recv.at[i, j],
            device_id=upper if j else lower, device_id_type=MESH,
        )

    for i, (array, view) in enumerate(kinds):
        for j, has in ((0, has_lower), (1, has_upper)):
            arrived(array, j, view(1 + j))

            @pl.when(has)
            def _():
                halo(i, j, view).start()

    for j in range(2):
        arrived(2, j, frame(kb, j))
        arrived(3, j, frame(vb, j))

    for j in range(2):
        kt[:, j * FRAME : (j + 1) * FRAME] = (
            kb[j * FRAME : (j + 1) * FRAME, :].astype(jnp.float32).T.astype(jnp.bfloat16)
        )
    dqt[...] = jnp.zeros_like(dqt)
    dka[...] = jnp.zeros_like(dka)
    dva[...] = jnp.zeros_like(dva)

    for i, (array, view) in enumerate(kinds):

        @pl.when(has_upper)
        def _():
            pltpu.make_async_remote_copy(
                view(3), view(3), halo_send.at[i, 0], halo_recv.at[i, 0], device_id=lower, device_id_type=MESH
            ).wait_recv()

        @pl.when(has_lower)
        def _():
            pltpu.make_async_remote_copy(
                view(0), view(0), halo_send.at[i, 1], halo_recv.at[i, 1], device_id=upper, device_id_type=MESH
            ).wait_recv()

    lane = lax.broadcasted_iota(jnp.int32, (8, HD), 1)

    def make_stats(s):
        deltas = []
        for group in range(4):
            p0, p1, p2, p3 = (dl[s, 4 * group + i] for i in range(4))
            r1, r2, r3 = (pltpu.roll(p, 128 - 32 * i, 1) for i, p in ((1, p1), (2, p2), (3, p3)))
            deltas.append(jnp.where(lane < 96, p0, r1))
            deltas.append(jnp.where(lane < 64, r1, r2))
            deltas.append(jnp.where(lane < 32, r2, r3))
        for t in range(12):
            cols = slice((t % 4) * HD, (t % 4 + 1) * HD)
            lse = ls[s, t : t + 1, :] * LOG2E
            stat[s, t // 4, 0:1, cols] = lse
            stat[s, t // 4, 1:2, cols] = deltas[t][0:1, :]
            stat[s, t // 4, 2:3, cols] = lse + bias[s, 0, t : t + 1, :]
            stat[s, t // 4, 3:4, cols] = lse + bias[s, 1, t : t + 1, :]

    make_stats(1)
    make_stats(2)

    @pl.when(has_lower)
    def _():
        make_stats(0)

    @pl.when(has_upper)
    def _():
        make_stats(3)

    def block(i, _):
        pair, row = i // ROWS, i % ROWS
        j = pair // 3
        s = j + pair % 3
        at = pl.ds(pl.multiple_of(s * FRAME + row * QROW, QROW), QROW)
        keys = pl.ds(pl.multiple_of(j * FRAME, FRAME), FRAME)
        queries, grads = qb[at, :], gb[at, :]
        scores = dot(kb[keys, :], queries, NT)
        grad_p = dot(vb[keys, :], grads, NT)
        rest = stat[s, row, 1:2, :]
        weights, score_grads = [], []
        for t in range(12):
            band = slice(t * HD, (t + 1) * HD)
            which = (2, 0, 0, 3)[t % 4]
            weight = jnp.exp2(scores[band] * (SCALE * LOG2E) - stat[s, row, which : which + 1, :])
            weights.append(weight.astype(jnp.bfloat16))
            score_grads.append((weight * (grad_p[band] - rest)).astype(jnp.bfloat16))
        weights = jnp.concatenate(weights, axis=0)
        score_grads = jnp.concatenate(score_grads, axis=0)
        dva[keys, :] += dot(weights, grads, NN)
        dka[keys, :] += dot(score_grads, queries, NN)
        dqt[:, at] += dot(kt[:, keys], score_grads, NN)
        return 0

    lax.fori_loop(
        jnp.where(has_lower, 0, ROWS), jnp.where(has_upper, 6 * ROWS, 5 * ROWS), block, 0
    )

    def send_part(side):
        return pltpu.make_async_remote_copy(
            part_src.at[side], part.at[1 - side], part_send.at[side], part_recv.at[1 - side],
            device_id=upper if side else lower, device_id_type=MESH,
        )

    for side, has in ((0, has_lower), (1, has_upper)):

        @pl.when(has)
        def _():
            at = slice(3 * side * FRAME, (3 * side + 1) * FRAME)
            part_src[side] = dqt[:, at].T.astype(jnp.bfloat16)
            send_part(side).start()

    def gather(array, src, out):
        def send(i, _):
            piece = (i + 7 * head) % 32
            pltpu.make_async_remote_copy(
                src.at[pl.ds(pl.multiple_of(piece * SLAB, 32), SLAB)], out.at[:, columns(head)],
                out_send.at[array], out_recv.at[array],
                device_id=source(piece // 16, piece % 16), device_id_type=MESH,
            ).start()
            return 0

        lax.fori_loop(0, 32, send, 0)

    ok[...] = (dka[...] * SCALE).astype(jnp.bfloat16)
    gather(1, ok, dk_out)
    ov[...] = dva[...].astype(jnp.bfloat16)
    gather(2, ov, dv_out)

    for j, has in ((0, has_lower), (1, has_upper)):
        at = slice((1 + j) * FRAME, (2 + j) * FRAME)
        own = slice(j * FRAME, (j + 1) * FRAME)

        @pl.when(has)
        def _():
            pltpu.make_async_remote_copy(
                part.at[j], part.at[j], part_send.at[j], part_recv.at[j], device_id=lower, device_id_type=MESH
            ).wait_recv()
            oq[own, :] = ((dqt[:, at].T + part[j].astype(jnp.float32)) * SCALE).astype(jnp.bfloat16)

        @pl.when(jnp.logical_not(has))
        def _():
            oq[own, :] = (dqt[:, at].T * SCALE).astype(jnp.bfloat16)

    gather(0, oq, dq_out)

    for array, view in ((0, qb), (1, gb), (2, kb), (3, vb)):
        whole = view.at[0 : 2 * FRAME]
        pltpu.make_async_remote_copy(
            whole, whole, in_send.at[array], in_recv.at[array, 0], device_id=lower, device_id_type=MESH
        ).wait_send()
    pltpu.make_async_remote_copy(
        dl_src, dl_src, in_send.at[4], in_recv.at[4, 0], device_id=lower, device_id_type=MESH
    ).wait_send()
    pltpu.make_async_remote_copy(
        lse_hbm, lse_hbm, in_send.at[5], in_recv.at[5, 0], device_id=lower, device_id_type=MESH
    ).wait_send()
    for j, has in ((0, has_lower), (1, has_upper)):

        @pl.when(has)
        def _():
            for i, (array, view) in enumerate(kinds):
                halo(i, j, view).wait_send()
            send_part(j).wait_send()

    for array, src, out in ((0, oq, dq_out), (1, ok, dk_out), (2, ov, dv_out)):
        pltpu.make_async_remote_copy(
            src, src, out_send.at[array], out_recv.at[array], device_id=lower, device_id_type=MESH
        ).wait_send()
        pltpu.make_async_remote_copy(
            out, out, out_send.at[array], out_recv.at[array], device_id=lower, device_id_type=MESH
        ).wait_recv()


def shards(queries, key_tokens, value_tokens, outputs, out_grad, log_sum, neighbours):
    tm, hd = lax.axis_index("tm"), lax.axis_index("head")
    place = 2 * (1 - tm // 4) + hd % 2
    lse_rows = log_sum.T.reshape(2, 12, HD)
    centre = neighbours[:, 13] % 4
    hide = jnp.stack([centre == 2, centre == 1]).astype(jnp.float32) * 1e30
    hide = jnp.pad(hide, ((0, 0), (12, 12)))
    hide = lax.dynamic_slice_in_dim(hide, 24 * place, 48, 1).reshape(2, 4, 12)
    bias = jnp.broadcast_to(hide.transpose(1, 0, 2)[..., None], (4, 2, 12, HD))
    bf16, f32 = jnp.bfloat16, jnp.float32
    anywhere, vmem = pl.BlockSpec(memory_space=pl.ANY), pl.BlockSpec(memory_space=pltpu.VMEM)
    dma = pltpu.SemaphoreType.DMA
    token_shape = jax.ShapeDtypeStruct(queries.shape, bf16)
    return tuple(
        pl.pallas_call(
            kernel,
            out_shape=[token_shape] * 3,
            in_specs=[anywhere] * 6 + [vmem],
            out_specs=[anywhere] * 3,
            scratch_shapes=[
                pltpu.VMEM((4 * FRAME, HD), bf16),
                pltpu.VMEM((4 * FRAME, HD), bf16),
                pltpu.VMEM((2 * FRAME, HD), bf16),
                pltpu.VMEM((2 * FRAME, HD), bf16),
                pltpu.VMEM((HD, 2 * FRAME), bf16),
                pltpu.VMEM((HD, 4 * FRAME), f32),
                pltpu.VMEM((2 * FRAME, HD), f32),
                pltpu.VMEM((2 * FRAME, HD), f32),
                pltpu.VMEM((4, ROWS, 8, QROW), f32),
                pltpu.VMEM((SLAB, HEADS * HD), bf16),
                pltpu.VMEM((SLAB, HEADS * HD), bf16),
                pltpu.VMEM((HEADS, 8, HD), f32),
                pltpu.VMEM((4, 16, 8, HD), f32),
                pltpu.VMEM((4, 12, HD), f32),
                pltpu.VMEM((2, FRAME, HD), bf16),
                pltpu.VMEM((2, FRAME, HD), bf16),
                pltpu.VMEM((2 * FRAME, HD), bf16),
                pltpu.VMEM((2 * FRAME, HD), bf16),
                pltpu.VMEM((2 * FRAME, HD), bf16),
                dma((2,)),
                dma((6,)),
                dma((6, 2)),
                dma((4, 2)),
                dma((4, 2)),
                dma((2,)),
                dma((2,)),
                dma((3,)),
                dma((3,)),
            ],
            compiler_params=pltpu.CompilerParams(
                collective_id=0, has_side_effects=True, vmem_limit_bytes=60 << 20
            ),
        )(queries, key_tokens, value_tokens, outputs, out_grad, lse_rows, bias)
    )


def solution(mesh):
    tokens = P(("tm", "head"), None)
    return jax.shard_map(
        shards,
        mesh=mesh,
        in_specs=(tokens, tokens, tokens, tokens, tokens, P("tm", "head"), P()),
        out_specs=(tokens, tokens, tokens),
        check_vma=False,
    )
```

```python
import functools

import jax
import jax.numpy as jnp
from jax import lax
from jax.experimental import pallas as pl
from jax.experimental.pallas import tpu as pltpu
from jax.sharding import PartitionSpec as P

HD = 128
FRAME = 1536
SLAB = 96
ROWS = 3
QROW = 512
HEADS = 32
LOG2E = 1.4426950408889634
SCALE = HD**-0.5
MESH = pl.DeviceIdType.MESH
NT = (((1,), (1,)), ((), ()))
NN = (((1,), (0,)), ((), ()))


def dot(left, right, dims):
    return lax.dot_general(left, right, dims, preferred_element_type=jnp.float32)


def kernel(
    q_hbm, k_hbm, v_hbm, o_hbm, g_hbm, lse_hbm, bias,
    dq_out, dk_out, dv_out,
    qb, gb, kb, vb, kt, dqt, dka, dva, stat, kept,
    ob, gl, dl_src, dl, ls, part_src, part, oq, ok, ov,
    load_sem, in_send, in_recv, halo_send, halo_recv, part_send, part_recv, out_send, out_recv,
):
    tm, hd = lax.axis_index("tm"), lax.axis_index("head")
    z_lo, x = tm // 4, tm % 4
    y, z_hi, core = hd // 4, (hd // 2) % 2, hd % 2
    place = 2 * (1 - z_lo) + core
    head = y * 8 + z_hi * 4 + x
    slot = tm % 2

    def holder(n):
        return ((1 - n // 2) * 4 + x, y * 4 + z_hi * 2 + n % 2)

    lower, upper = holder((place + 3) % 4), holder((place + 1) % 4)
    has_lower, has_upper = place > 0, place < 3

    def target(h):
        return ((1 - z_lo) * 4 + h % 4, (h // 8) * 4 + ((h // 4) % 2) * 2 + x // 2)

    def source(j, s):
        return (2 * place + j, s)

    load_o = pltpu.make_async_copy(o_hbm, ob, load_sem.at[0])
    load_g = pltpu.make_async_copy(g_hbm, gl, load_sem.at[1])
    load_o.start()
    load_g.start()

    barrier = pltpu.get_barrier_semaphore()

    def greet(i, _):
        pl.semaphore_signal(barrier, inc=1, device_id=source(i // 16, i % 16), device_id_type=MESH)
        return 0

    lax.fori_loop(0, 32, greet, 0)
    for peer in (lower, upper):
        pl.semaphore_signal(barrier, inc=1, device_id=peer, device_id_type=MESH)
    pl.semaphore_wait(barrier, 34)

    def columns(h):
        return pl.ds(pl.multiple_of(h * HD, HD), HD)

    first = (slot * 16 + hd) * 5

    def spread(array, src, dst, row):
        def send(i, _):
            h = (i + first) % HEADS
            pltpu.make_async_remote_copy(
                src.at[:, columns(h)],
                dst.at[pl.ds(pl.multiple_of(row, 32), SLAB)],
                in_send.at[array], in_recv.at[array, slot],
                device_id=target(h), device_id_type=MESH,
            ).start()
            return 0

        lax.fori_loop(0, HEADS, send, 0)

    own_row = (1 + slot) * FRAME + hd * SLAB
    kv_row = slot * FRAME + hd * SLAB
    spread(0, q_hbm, qb, own_row)
    for i in range(2):
        pltpu.make_async_remote_copy(
            lse_hbm.at[i], ls.at[1 + slot], in_send.at[5], in_recv.at[5, slot],
            device_id=target(2 * hd + i), device_id_type=MESH,
        ).start()
    spread(1, g_hbm, gb, own_row)

    load_o.wait()
    load_g.wait()

    def delta(h, _):
        product = ob[:, columns(h)].astype(jnp.float32) * gl[:, columns(h)].astype(jnp.float32)
        tall = jnp.concatenate([product, jnp.zeros((HD - SLAB, HD), jnp.float32)], axis=0)
        row = jnp.sum(tall.T, axis=0, keepdims=True)
        dl_src[h] = jnp.broadcast_to(row, (8, HD))
        return 0

    lax.fori_loop(0, HEADS, delta, 0)

    def send_delta(i, _):
        h = (i + first) % HEADS
        pltpu.make_async_remote_copy(
            dl_src.at[h], dl.at[1 + slot, hd], in_send.at[4], in_recv.at[4, slot],
            device_id=target(h), device_id_type=MESH,
        ).start()
        return 0

    lax.fori_loop(0, HEADS, send_delta, 0)

    def frame(ref, j):
        return ref.at[j * FRAME : (j + 1) * FRAME]

    kinds = {
        0: lambda s: frame(qb, s),
        1: lambda s: frame(gb, s),
        4: lambda s: dl.at[s],
        5: lambda s: ls.at[s],
    }

    def arrived(array, j, view):
        pltpu.make_async_remote_copy(
            view, view, in_send.at[array], in_recv.at[array, j], device_id=lower, device_id_type=MESH
        ).wait_recv()

    def halo(array, j):
        view = kinds[array]
        return pltpu.make_async_remote_copy(
            view(1 + j), view(3 - 3 * j), halo_send.at[array, j], halo_recv.at[array, j],
            device_id=upper if j else lower, device_id_type=MESH,
        )

    sides = ((0, has_lower), (1, has_upper))

    def forward(array):
        for j, has in sides:
            arrived(array, j, kinds[array](1 + j))

            @pl.when(has)
            def _():
                halo(array, j).start()

    def halo_arrived(array):
        for j, has in sides:

            @pl.when(has)
            def _():
                view = kinds[array](3 * j)
                pltpu.make_async_remote_copy(
                    view, view, halo_send.at[array, 1 - j], halo_recv.at[array, 1 - j],
                    device_id=lower, device_id_type=MESH,
                ).wait_recv()

    dqt[...] = jnp.zeros_like(dqt)
    dka[...] = jnp.zeros_like(dka)
    dva[...] = jnp.zeros_like(dva)

    lane = lax.broadcasted_iota(jnp.int32, (8, HD), 1)

    def lse_stats(s):
        for t in range(12):
            cols = slice((t % 4) * HD, (t % 4 + 1) * HD)
            lse = ls[s, t : t + 1, :] * LOG2E
            stat[s, t // 4, 0:1, cols] = lse
            stat[s, t // 4, 2:3, cols] = lse + bias[s, 0, t : t + 1, :]
            stat[s, t // 4, 3:4, cols] = lse + bias[s, 1, t : t + 1, :]

    def delta_stats(s):
        deltas = []
        for group in range(4):
            p0, p1, p2, p3 = (dl[s, 4 * group + i] for i in range(4))
            r1, r2, r3 = (pltpu.roll(p, 128 - 32 * i, 1) for i, p in ((1, p1), (2, p2), (3, p3)))
            deltas.append(jnp.where(lane < 96, p0, r1))
            deltas.append(jnp.where(lane < 64, r1, r2))
            deltas.append(jnp.where(lane < 32, r2, r3))
        for t in range(12):
            cols = slice((t % 4) * HD, (t % 4 + 1) * HD)
            stat[s, t // 4, 1:2, cols] = deltas[t][0:1, :]

    def at_rows(s, row):
        return pl.ds(pl.multiple_of(s * FRAME + row * QROW, QROW), QROW)

    def at_keys(j):
        return pl.ds(pl.multiple_of(j * FRAME, FRAME), FRAME)

    def at_kept(j, s):
        return pl.ds(pl.multiple_of((2 * j + s) * FRAME, FRAME), FRAME)

    def at_lanes(row):
        return pl.ds(pl.multiple_of(row * QROW, QROW), QROW)

    def weigh(j, s, row):
        scores = dot(kb[at_keys(j), :], qb[at_rows(s, row), :], NT)
        weights = []
        for t in range(12):
            which = (2, 0, 0, 3)[t % 4]
            shifted = scores[t * HD : (t + 1) * HD] * (SCALE * LOG2E) - stat[s, row, which : which + 1, :]
            weights.append(jnp.exp2(shifted).astype(jnp.bfloat16))
        kept[at_kept(j, s), at_lanes(row)] = jnp.concatenate(weights, axis=0)

    def value_terms(j, s):
        grads = gb[pl.ds(pl.multiple_of(s * FRAME, FRAME), FRAME), :]
        dva[at_keys(j), :] += dot(kept[at_kept(j, s), :], grads, NN)

    def score_terms(j, s, row):
        queries = qb[at_rows(s, row), :]
        grad_p = dot(vb[at_keys(j), :], gb[at_rows(s, row), :], NT)
        weights = kept[at_kept(j, s), at_lanes(row)].astype(jnp.float32)
        score_grads = (weights * (grad_p - stat[s, row, 1:2, :])).astype(jnp.bfloat16)
        dka[at_keys(j), :] += dot(score_grads, queries, NN)
        dqt[:, at_rows(s, row)] += dot(kt[:, at_keys(j)], score_grads, NN)

    def each(count, step):
        def body(i, _):
            step(i)
            return 0

        lax.fori_loop(0, count, body, 0)

    def on_halo(step):
        for j, has in sides:

            @pl.when(has)
            def _():
                step(j, 3 * j)

    def on_rows(term, j, s):
        each(ROWS, lambda row: term(j, s, row))

    def send_part(side):
        return pltpu.make_async_remote_copy(
            part_src.at[side], part.at[1 - side], part_send.at[side], part_recv.at[1 - side],
            device_id=upper if side else lower, device_id_type=MESH,
        )

    def gather(array, j, src, out):
        def send(i):
            piece = (i + head) % 16
            pltpu.make_async_remote_copy(
                src.at[pl.ds(pl.multiple_of(j * FRAME + piece * SLAB, 32), SLAB)], out.at[:, columns(head)],
                out_send.at[array], out_recv.at[array],
                device_id=source(j, piece), device_id_type=MESH,
            ).start()

        each(16, send)

    def own(j):
        return slice(j * FRAME, (j + 1) * FRAME)

    def finish_keys(j):
        ok[own(j), :] = (dka[own(j), :] * SCALE).astype(jnp.bfloat16)
        gather(1, j, ok, dk_out)

    def finish_queries(j, has):
        at = slice((1 + j) * FRAME, (2 + j) * FRAME)

        @pl.when(has)
        def _():
            pltpu.make_async_remote_copy(
                part.at[j], part.at[j], part_send.at[j], part_recv.at[j], device_id=lower, device_id_type=MESH
            ).wait_recv()
            oq[own(j), :] = ((dqt[:, at].T + part[j].astype(jnp.float32)) * SCALE).astype(jnp.bfloat16)

        @pl.when(jnp.logical_not(has))
        def _():
            oq[own(j), :] = (dqt[:, at].T * SCALE).astype(jnp.bfloat16)

        gather(0, j, oq, dq_out)

    forward(0)
    forward(5)
    spread(2, k_hbm, kb, kv_row)
    forward(1)
    forward(4)
    spread(3, v_hbm, vb, kv_row)
    lse_stats(1)
    lse_stats(2)
    for j in range(2):
        arrived(2, j, frame(kb, j))
    each(12, lambda i: weigh(i // 6, 1 + i // 3 % 2, i % 3))
    halo_arrived(0)
    halo_arrived(5)

    def halo_weights(j, s):
        lse_stats(s)
        on_rows(weigh, j, s)

    on_halo(halo_weights)
    for j in range(2):
        kt[:, own(j)] = kb[own(j), :].astype(jnp.float32).T.astype(jnp.bfloat16)

    delta_stats(1)
    delta_stats(2)
    each(4, lambda i: value_terms(i // 2, 1 + i % 2))
    halo_arrived(1)
    halo_arrived(4)
    on_halo(value_terms)
    ov[...] = dva[...].astype(jnp.bfloat16)
    gather(2, 0, ov, dv_out)

    for j in range(2):
        arrived(3, j, frame(vb, j))

    def halo_scores(j, s):
        delta_stats(s)
        on_rows(score_terms, j, s)
        part_src[j] = dqt[:, s * FRAME : (s + 1) * FRAME].T.astype(jnp.bfloat16)
        send_part(j).start()

    on_halo(halo_scores)
    gather(2, 1, ov, dv_out)
    each(6, lambda i: score_terms(0, 1 + i // 3, i % 3))
    finish_keys(0)
    on_rows(score_terms, 1, 1)
    finish_queries(0, has_lower)
    on_rows(score_terms, 1, 2)
    finish_keys(1)
    finish_queries(1, has_upper)

    for array, view in ((0, qb), (1, gb), (2, kb), (3, vb)):
        whole = view.at[0 : 2 * FRAME]
        pltpu.make_async_remote_copy(
            whole, whole, in_send.at[array], in_recv.at[array, 0], device_id=lower, device_id_type=MESH
        ).wait_send()
    pltpu.make_async_remote_copy(
        dl_src, dl_src, in_send.at[4], in_recv.at[4, 0], device_id=lower, device_id_type=MESH
    ).wait_send()
    pltpu.make_async_remote_copy(
        lse_hbm, lse_hbm, in_send.at[5], in_recv.at[5, 0], device_id=lower, device_id_type=MESH
    ).wait_send()
    for j, has in ((0, has_lower), (1, has_upper)):

        @pl.when(has)
        def _():
            for array in kinds:
                halo(array, j).wait_send()
            send_part(j).wait_send()

    for array, src, out in ((0, oq, dq_out), (1, ok, dk_out), (2, ov, dv_out)):
        pltpu.make_async_remote_copy(
            src, src, out_send.at[array], out_recv.at[array], device_id=lower, device_id_type=MESH
        ).wait_send()
        pltpu.make_async_remote_copy(
            out, out, out_send.at[array], out_recv.at[array], device_id=lower, device_id_type=MESH
        ).wait_recv()


def shards(queries, key_tokens, value_tokens, outputs, out_grad, log_sum, neighbours):
    tm, hd = lax.axis_index("tm"), lax.axis_index("head")
    place = 2 * (1 - tm // 4) + hd % 2
    lse_rows = log_sum.T.reshape(2, 12, HD)
    centre = neighbours[:, 13] % 4
    hide = jnp.stack([centre == 2, centre == 1]).astype(jnp.float32) * 1e30
    hide = jnp.pad(hide, ((0, 0), (12, 12)))
    hide = lax.dynamic_slice_in_dim(hide, 24 * place, 48, 1).reshape(2, 4, 12)
    bias = jnp.broadcast_to(hide.transpose(1, 0, 2)[..., None], (4, 2, 12, HD))
    bf16, f32 = jnp.bfloat16, jnp.float32
    anywhere, vmem = pl.BlockSpec(memory_space=pl.ANY), pl.BlockSpec(memory_space=pltpu.VMEM)
    dma = pltpu.SemaphoreType.DMA
    token_shape = jax.ShapeDtypeStruct(queries.shape, bf16)
    return tuple(
        pl.pallas_call(
            kernel,
            out_shape=[token_shape] * 3,
            in_specs=[anywhere] * 6 + [vmem],
            out_specs=[anywhere] * 3,
            scratch_shapes=[
                pltpu.VMEM((4 * FRAME, HD), bf16),
                pltpu.VMEM((4 * FRAME, HD), bf16),
                pltpu.VMEM((2 * FRAME, HD), bf16),
                pltpu.VMEM((2 * FRAME, HD), bf16),
                pltpu.VMEM((HD, 2 * FRAME), bf16),
                pltpu.VMEM((HD, 4 * FRAME), f32),
                pltpu.VMEM((2 * FRAME, HD), f32),
                pltpu.VMEM((2 * FRAME, HD), f32),
                pltpu.VMEM((4, ROWS, 8, QROW), f32),
                pltpu.VMEM((6 * FRAME, FRAME), bf16),
                pltpu.VMEM((SLAB, HEADS * HD), bf16),
                pltpu.VMEM((SLAB, HEADS * HD), bf16),
                pltpu.VMEM((HEADS, 8, HD), f32),
                pltpu.VMEM((4, 16, 8, HD), f32),
                pltpu.VMEM((4, 12, HD), f32),
                pltpu.VMEM((2, FRAME, HD), bf16),
                pltpu.VMEM((2, FRAME, HD), bf16),
                pltpu.VMEM((2 * FRAME, HD), bf16),
                pltpu.VMEM((2 * FRAME, HD), bf16),
                pltpu.VMEM((2 * FRAME, HD), bf16),
                dma((2,)),
                dma((6,)),
                dma((6, 2)),
                dma((6, 2)),
                dma((6, 2)),
                dma((2,)),
                dma((2,)),
                dma((3,)),
                dma((3,)),
            ],
            compiler_params=pltpu.CompilerParams(
                collective_id=0, has_side_effects=True, vmem_limit_bytes=67043328
            ),
        )(queries, key_tokens, value_tokens, outputs, out_grad, lse_rows, bias)
    )


def solution(mesh):
    tokens = P(("tm", "head"), None)
    return jax.shard_map(
        shards,
        mesh=mesh,
        in_specs=(tokens, tokens, tokens, tokens, tokens, P("tm", "head"), P()),
        out_specs=(tokens, tokens, tokens),
        check_vma=False,
    )
```

```python
import functools

import jax
import jax.numpy as jnp
from jax import lax
from jax.experimental import pallas as pl
from jax.experimental.pallas import tpu as pltpu
from jax.sharding import PartitionSpec as P

HD = 128
FRAME = 1536
SLAB = 96
ROWS = 3
QROW = 512
HEADS = 32
LOG2E = 1.4426950408889634
SCALE = HD**-0.5
MESH = pl.DeviceIdType.MESH
NT = (((1,), (1,)), ((), ()))
NN = (((1,), (0,)), ((), ()))


def dot(left, right, dims):
    return lax.dot_general(left, right, dims, preferred_element_type=jnp.float32)


def kernel(
    q_hbm, k_hbm, v_hbm, o_hbm, g_hbm, lse_hbm, listed,
    dq_out, dk_out, dv_out,
    qb, gb, kb, vb, kt, dqt, dka, dva, stat, kept,
    ob, gl, dl_src, dl, ls, part_src, part, oq, ok, ov,
    load_sem, in_send, in_recv, halo_send, halo_recv, part_send, part_recv, out_send, out_recv,
):
    tm, hd = lax.axis_index("tm"), lax.axis_index("head")
    z_lo, x = tm // 4, tm % 4
    y, z_hi, core = hd // 4, (hd // 2) % 2, hd % 2
    place = 2 * (1 - z_lo) + core
    head = y * 8 + z_hi * 4 + x
    slot = tm % 2

    def holder(n):
        return ((1 - n // 2) * 4 + x, y * 4 + z_hi * 2 + n % 2)

    lower, upper = holder((place + 3) % 4), holder((place + 1) % 4)
    has_lower, has_upper = place > 0, place < 3

    def target(h):
        return ((1 - z_lo) * 4 + h % 4, (h // 8) * 4 + ((h // 4) % 2) * 2 + x // 2)

    def source(j, s):
        return (2 * place + j, s)

    load_o = pltpu.make_async_copy(o_hbm, ob, load_sem.at[0])
    load_g = pltpu.make_async_copy(g_hbm, gl, load_sem.at[1])
    load_o.start()
    load_g.start()

    barrier = pltpu.get_barrier_semaphore()

    def greet(i, _):
        pl.semaphore_signal(barrier, inc=1, device_id=source(i // 16, i % 16), device_id_type=MESH)
        return 0

    lax.fori_loop(0, 32, greet, 0)
    for peer in (lower, upper):
        pl.semaphore_signal(barrier, inc=1, device_id=peer, device_id_type=MESH)
    pl.semaphore_wait(barrier, 34)

    def columns(h):
        return pl.ds(pl.multiple_of(h * HD, HD), HD)

    first = (slot * 16 + hd) * 5

    def spread(array, src, dst, row):
        def send(i, _):
            h = (i + first) % HEADS
            pltpu.make_async_remote_copy(
                src.at[:, columns(h)],
                dst.at[pl.ds(pl.multiple_of(row, 32), SLAB)],
                in_send.at[array], in_recv.at[array, slot],
                device_id=target(h), device_id_type=MESH,
            ).start()
            return 0

        lax.fori_loop(0, HEADS, send, 0)

    own_row = (1 + slot) * FRAME + hd * SLAB
    kv_row = slot * FRAME + hd * SLAB
    spread(0, q_hbm, qb, own_row)
    for i in range(2):
        pltpu.make_async_remote_copy(
            lse_hbm.at[i], ls.at[1 + slot], in_send.at[5], in_recv.at[5, slot],
            device_id=target(2 * hd + i), device_id_type=MESH,
        ).start()
    spread(1, g_hbm, gb, own_row)

    load_o.wait()
    load_g.wait()

    def delta(h, _):
        product = ob[:, columns(h)].astype(jnp.float32) * gl[:, columns(h)].astype(jnp.float32)
        tall = jnp.concatenate([product, jnp.zeros((HD - SLAB, HD), jnp.float32)], axis=0)
        row = jnp.sum(tall.T, axis=0, keepdims=True)
        dl_src[h] = jnp.broadcast_to(row, (8, HD))
        return 0

    lax.fori_loop(0, HEADS, delta, 0)

    def send_delta(i, _):
        h = (i + first) % HEADS
        pltpu.make_async_remote_copy(
            dl_src.at[h], dl.at[1 + slot, hd], in_send.at[4], in_recv.at[4, slot],
            device_id=target(h), device_id_type=MESH,
        ).start()
        return 0

    lax.fori_loop(0, HEADS, send_delta, 0)

    def frame(ref, j):
        return ref.at[j * FRAME : (j + 1) * FRAME]

    kinds = {
        0: lambda s: frame(qb, s),
        1: lambda s: frame(gb, s),
        4: lambda s: dl.at[s],
        5: lambda s: ls.at[s],
    }

    def arrived(array, j, view):
        pltpu.make_async_remote_copy(
            view, view, in_send.at[array], in_recv.at[array, j], device_id=lower, device_id_type=MESH
        ).wait_recv()

    def halo(array, j):
        view = kinds[array]
        return pltpu.make_async_remote_copy(
            view(1 + j), view(3 - 3 * j), halo_send.at[array, j], halo_recv.at[array, j],
            device_id=upper if j else lower, device_id_type=MESH,
        )

    sides = ((0, has_lower), (1, has_upper))

    def forward(array):
        for j, has in sides:
            arrived(array, j, kinds[array](1 + j))

            @pl.when(has)
            def _():
                halo(array, j).start()

    def halo_arrived(array):
        for j, has in sides:

            @pl.when(has)
            def _():
                view = kinds[array](3 * j)
                pltpu.make_async_remote_copy(
                    view, view, halo_send.at[array, 1 - j], halo_recv.at[array, 1 - j],
                    device_id=lower, device_id_type=MESH,
                ).wait_recv()

    dqt[...] = jnp.zeros_like(dqt)
    dka[...] = jnp.zeros_like(dka)
    dva[...] = jnp.zeros_like(dva)

    lane = lax.broadcasted_iota(jnp.int32, (8, HD), 1)

    def lse_stats(s):
        for t in range(12):
            cols = slice((t % 4) * HD, (t % 4 + 1) * HD)
            lse = ls[s, t : t + 1, :] * LOG2E
            stat[s, t // 4, 0:1, cols] = lse
            centre = listed[(2 * place - 1 + s) * 12 + t, 13] % 4
            stat[s, t // 4, 2:3, cols] = lse + jnp.where(centre == 2, 1e30, 0.0)
            stat[s, t // 4, 3:4, cols] = lse + jnp.where(centre == 1, 1e30, 0.0)

    def delta_stats(s):
        deltas = []
        for group in range(4):
            p0, p1, p2, p3 = (dl[s, 4 * group + i] for i in range(4))
            r1, r2, r3 = (pltpu.roll(p, 128 - 32 * i, 1) for i, p in ((1, p1), (2, p2), (3, p3)))
            deltas.append(jnp.where(lane < 96, p0, r1))
            deltas.append(jnp.where(lane < 64, r1, r2))
            deltas.append(jnp.where(lane < 32, r2, r3))
        for t in range(12):
            cols = slice((t % 4) * HD, (t % 4 + 1) * HD)
            stat[s, t // 4, 1:2, cols] = deltas[t][0:1, :]

    def at_rows(s, row):
        return pl.ds(pl.multiple_of(s * FRAME + row * QROW, QROW), QROW)

    def at_keys(j):
        return pl.ds(pl.multiple_of(j * FRAME, FRAME), FRAME)

    def at_kept(j, s):
        return pl.ds(pl.multiple_of((2 * j + s) * FRAME, FRAME), FRAME)

    def at_lanes(row):
        return pl.ds(pl.multiple_of(row * QROW, QROW), QROW)

    def weigh(j, s, row):
        scores = dot(kb[at_keys(j), :], qb[at_rows(s, row), :], NT)
        weights = []
        for t in range(12):
            which = (2, 0, 0, 3)[t % 4]
            shifted = scores[t * HD : (t + 1) * HD] * (SCALE * LOG2E) - stat[s, row, which : which + 1, :]
            weights.append(jnp.exp2(shifted).astype(jnp.bfloat16))
        kept[at_kept(j, s), at_lanes(row)] = jnp.concatenate(weights, axis=0)

    def value_terms(j, s):
        grads = gb[pl.ds(pl.multiple_of(s * FRAME, FRAME), FRAME), :]
        dva[at_keys(j), :] += dot(kept[at_kept(j, s), :], grads, NN)

    def score_terms(j, s, row):
        queries = qb[at_rows(s, row), :]
        grad_p = dot(vb[at_keys(j), :], gb[at_rows(s, row), :], NT)
        weights = kept[at_kept(j, s), at_lanes(row)].astype(jnp.float32)
        score_grads = (weights * (grad_p - stat[s, row, 1:2, :])).astype(jnp.bfloat16)
        dka[at_keys(j), :] += dot(score_grads, queries, NN)
        dqt[:, at_rows(s, row)] += dot(kt[:, at_keys(j)], score_grads, NN)

    def each(count, step):
        def body(i, _):
            step(i)
            return 0

        lax.fori_loop(0, count, body, 0)

    def on_halo(step):
        for j, has in sides:

            @pl.when(has)
            def _():
                step(j, 3 * j)

    def on_rows(term, j, s):
        each(ROWS, lambda row: term(j, s, row))

    def send_part(side):
        return pltpu.make_async_remote_copy(
            part_src.at[side], part.at[1 - side], part_send.at[side], part_recv.at[1 - side],
            device_id=upper if side else lower, device_id_type=MESH,
        )

    def gather(array, j, src, out):
        def send(i):
            piece = (i + head) % 16
            pltpu.make_async_remote_copy(
                src.at[pl.ds(pl.multiple_of(j * FRAME + piece * SLAB, 32), SLAB)], out.at[:, columns(head)],
                out_send.at[array], out_recv.at[array],
                device_id=source(j, piece), device_id_type=MESH,
            ).start()

        each(16, send)

    def own(j):
        return slice(j * FRAME, (j + 1) * FRAME)

    def finish_keys(j):
        ok[own(j), :] = (dka[own(j), :] * SCALE).astype(jnp.bfloat16)
        gather(1, j, ok, dk_out)

    def finish_queries(j, has):
        at = slice((1 + j) * FRAME, (2 + j) * FRAME)

        @pl.when(has)
        def _():
            pltpu.make_async_remote_copy(
                part.at[j], part.at[j], part_send.at[j], part_recv.at[j], device_id=lower, device_id_type=MESH
            ).wait_recv()
            oq[own(j), :] = ((dqt[:, at].T + part[j].astype(jnp.float32)) * SCALE).astype(jnp.bfloat16)

        @pl.when(jnp.logical_not(has))
        def _():
            oq[own(j), :] = (dqt[:, at].T * SCALE).astype(jnp.bfloat16)

        gather(0, j, oq, dq_out)

    forward(0)
    forward(5)
    spread(2, k_hbm, kb, kv_row)
    forward(1)
    forward(4)
    spread(3, v_hbm, vb, kv_row)
    lse_stats(1)
    lse_stats(2)
    for j in range(2):
        arrived(2, j, frame(kb, j))
    each(12, lambda i: weigh(i // 6, 1 + i // 3 % 2, i % 3))
    halo_arrived(0)
    halo_arrived(5)

    def halo_weights(j, s):
        lse_stats(s)
        on_rows(weigh, j, s)

    on_halo(halo_weights)
    for j in range(2):
        kt[:, own(j)] = kb[own(j), :].astype(jnp.float32).T.astype(jnp.bfloat16)

    delta_stats(1)
    delta_stats(2)
    each(4, lambda i: value_terms(i // 2, 1 + i % 2))
    halo_arrived(1)
    halo_arrived(4)
    on_halo(value_terms)
    ov[...] = dva[...].astype(jnp.bfloat16)
    gather(2, 0, ov, dv_out)

    for j in range(2):
        arrived(3, j, frame(vb, j))

    def halo_scores(j, s):
        delta_stats(s)
        on_rows(score_terms, j, s)
        part_src[j] = dqt[:, s * FRAME : (s + 1) * FRAME].T.astype(jnp.bfloat16)
        send_part(j).start()

    on_halo(halo_scores)
    gather(2, 1, ov, dv_out)
    each(6, lambda i: score_terms(0, 1 + i // 3, i % 3))
    finish_keys(0)
    on_rows(score_terms, 1, 1)
    finish_queries(0, has_lower)
    on_rows(score_terms, 1, 2)
    finish_keys(1)
    finish_queries(1, has_upper)

    for array, view in ((0, qb), (1, gb), (2, kb), (3, vb)):
        whole = view.at[0 : 2 * FRAME]
        pltpu.make_async_remote_copy(
            whole, whole, in_send.at[array], in_recv.at[array, 0], device_id=lower, device_id_type=MESH
        ).wait_send()
    pltpu.make_async_remote_copy(
        dl_src, dl_src, in_send.at[4], in_recv.at[4, 0], device_id=lower, device_id_type=MESH
    ).wait_send()
    pltpu.make_async_remote_copy(
        lse_hbm, lse_hbm, in_send.at[5], in_recv.at[5, 0], device_id=lower, device_id_type=MESH
    ).wait_send()
    for j, has in ((0, has_lower), (1, has_upper)):

        @pl.when(has)
        def _():
            for array in kinds:
                halo(array, j).wait_send()
            send_part(j).wait_send()

    for array, src, out in ((0, oq, dq_out), (1, ok, dk_out), (2, ov, dv_out)):
        pltpu.make_async_remote_copy(
            src, src, out_send.at[array], out_recv.at[array], device_id=lower, device_id_type=MESH
        ).wait_send()
        pltpu.make_async_remote_copy(
            out, out, out_send.at[array], out_recv.at[array], device_id=lower, device_id_type=MESH
        ).wait_recv()


def shards(queries, key_tokens, value_tokens, outputs, out_grad, log_sum, neighbours):
    lse_rows = log_sum.T.reshape(2, 12, HD)
    bf16, f32 = jnp.bfloat16, jnp.float32
    anywhere = pl.BlockSpec(memory_space=pl.ANY)
    dma = pltpu.SemaphoreType.DMA
    token_shape = jax.ShapeDtypeStruct(queries.shape, bf16)
    return tuple(
        pl.pallas_call(
            kernel,
            out_shape=[token_shape] * 3,
            in_specs=[anywhere] * 6 + [pl.BlockSpec(memory_space=pltpu.SMEM)],
            out_specs=[anywhere] * 3,
            scratch_shapes=[
                pltpu.VMEM((4 * FRAME, HD), bf16),
                pltpu.VMEM((4 * FRAME, HD), bf16),
                pltpu.VMEM((2 * FRAME, HD), bf16),
                pltpu.VMEM((2 * FRAME, HD), bf16),
                pltpu.VMEM((HD, 2 * FRAME), bf16),
                pltpu.VMEM((HD, 4 * FRAME), f32),
                pltpu.VMEM((2 * FRAME, HD), f32),
                pltpu.VMEM((2 * FRAME, HD), f32),
                pltpu.VMEM((4, ROWS, 8, QROW), f32),
                pltpu.VMEM((6 * FRAME, FRAME), bf16),
                pltpu.VMEM((SLAB, HEADS * HD), bf16),
                pltpu.VMEM((SLAB, HEADS * HD), bf16),
                pltpu.VMEM((HEADS, 8, HD), f32),
                pltpu.VMEM((4, 16, 8, HD), f32),
                pltpu.VMEM((4, 12, HD), f32),
                pltpu.VMEM((2, FRAME, HD), bf16),
                pltpu.VMEM((2, FRAME, HD), bf16),
                pltpu.VMEM((2 * FRAME, HD), bf16),
                pltpu.VMEM((2 * FRAME, HD), bf16),
                pltpu.VMEM((2 * FRAME, HD), bf16),
                dma((2,)),
                dma((6,)),
                dma((6, 2)),
                dma((6, 2)),
                dma((6, 2)),
                dma((2,)),
                dma((2,)),
                dma((3,)),
                dma((3,)),
            ],
            compiler_params=pltpu.CompilerParams(
                collective_id=0, has_side_effects=True, vmem_limit_bytes=67043328
            ),
        )(queries, key_tokens, value_tokens, outputs, out_grad, lse_rows, neighbours)
    )


def solution(mesh):
    tokens = P(("tm", "head"), None)
    return jax.shard_map(
        shards,
        mesh=mesh,
        in_specs=(tokens, tokens, tokens, tokens, tokens, P("tm", "head"), P()),
        out_specs=(tokens, tokens, tokens),
        check_vma=False,
    )
```
